32 devices in a mesh: row: 16 (over z, y, core), col: 2 (over x).
Axes of the slice: x: 2, y: 2, z: 4, core: 2. Of those that a mesh axis runs over, the one named last changes fastest.
Arguments:
- c_matrix: bfloat16 [2, 3072, 6144], P(None, 'row', 'col'), may hold values from -6 to 6
- beta_values: bfloat16 [1, 48, 6, 128, 128], P(None, 'col'), may hold values from -0.21875 to 0.21875
- beta_rows: int32 [1, 48, 6], P(None, 'col'), may hold values from 0 to 47, as said below
- alpha_values: bfloat16 [1, 2, 16, 4, 192, 192], P(None, None, 'row'), may hold values from -0.21875 to 0.21875
- alpha_rows: int32 [1, 2, 16, 4], P(None, None, 'row'), may hold values from 0 to 31, as said below
- gaps: float32 [2, 3072, 6144], P(None, 'row', 'col'), may hold values from 0.5 to 4
Outputs:
- update: float32 [2, 3072, 6144], P(None, 'row', 'col')
The draws below stay inside these ranges and needn't reach their ends.
Inputs may be any that keep to these rules, and one draw needn't show every extreme that they name: For every k and tile column j, beta_rows[k, j] lists 6 distinct tile rows and its first entry is j. For every k, g, r, alpha_rows[k, g, r] lists 4 distinct tile rows and its first entry is the tile column g * 16 + r.
All inputs are finite; a program needn't handle non-finite values.
Results may differ from the reference program's by a relative error of at most 0.0029.
Values may be sent and summed in bfloat16 or wider, within the bound.
A program may use at most 192 MiB of HBM per device.

```python
import math
import jax
import jax.numpy as jnp
from jax import lax

ORDER = 6144
PAIRS = 1
TILE_B = 128
GROUPS = 2
SPAN = 3072
ATILE = 192
ROWTILES = 16
BTILES = 48
BNZ = 6
ATILES = 32
ANZ = 4


def tile_lists(key, operators, tile_total, listed):
    scores = jax.random.randint(key, (operators, tile_total, tile_total), 0, 1 << 20) * tile_total
    scores = scores + jnp.arange(tile_total, dtype=jnp.int32)
    scores = jnp.where(jnp.eye(tile_total, dtype=bool)[None], -1, scores)
    return jnp.argsort(scores, axis=-1)[..., :listed].astype(jnp.int32)


def draw_beta_rows(key, part):
    return tile_lists(jax.random.fold_in(key, 11), PAIRS, BTILES, BNZ)


def draw_alpha_rows(key, part):
    tile_table = tile_lists(jax.random.fold_in(key, 23), PAIRS, ATILES, ANZ)
    return tile_table.reshape(PAIRS, GROUPS, ROWTILES, ANZ)


def shard_levels(own_key, shape, pieces, low, top_value):
    def one(dim, blocks):
        steps = jax.random.uniform(jax.random.fold_in(jax.random.fold_in(own_key, 6), dim), (blocks,), jnp.float32, low / len(pieces), top_value / len(pieces))
        return jnp.repeat(jnp.exp(steps), shape[dim] // blocks).reshape((-1,) + (1,) * (len(shape) - dim - 1))

    level = one(*pieces[0])
    for cut in pieces[1:]:
        level = level * one(*cut)
    return level


def centred(own_key, shape, spread, reach, pieces=(), kind=jnp.bfloat16):
    drawn = jax.random.normal(own_key, shape, jnp.float32) * spread
    if len(pieces) > 0:
        drawn = shard_levels(own_key, shape, pieces, -0.22, 0.18) * drawn
    return jnp.clip(drawn, min=-reach, max=reach).astype(kind)


def setup_inputs(seed: int = 0) -> dict:
    keys = jax.random.split(jax.random.key(seed), 7)
    return {
        "c_matrix": centred(keys[0], (GROUPS, SPAN, ORDER), 1.0, 6.0, ((1, 16), (2, 2))),
        "beta_values": centred(keys[1], (PAIRS, BTILES, BNZ, TILE_B, TILE_B), (BNZ * TILE_B) ** -0.5, 0.21875, ((1, 2),)),
        "beta_rows": draw_beta_rows(jax.random.fold_in(keys[6], 71), 0),
        "alpha_values": centred(keys[3], (PAIRS, GROUPS, ROWTILES, ANZ, ATILE, ATILE), (ANZ * ATILE) ** -0.5, 0.21875, ((2, 16),)),
        "alpha_rows": draw_alpha_rows(jax.random.fold_in(keys[6], 71), 0),
        "gaps": jnp.clip(jnp.exp(math.log(4.0) - 2.0794415 * jax.random.uniform(keys[5], (GROUPS, SPAN, ORDER), jnp.float32) ** shard_levels(keys[5], (GROUPS, SPAN, ORDER), ((1, 16), (2, 2)), -0.2, 0.2)), 0.5, 4.0),
    }


def reference(c_matrix, beta_values, beta_rows, alpha_values, alpha_rows, gaps):
    c_full = c_matrix.reshape(ORDER, ORDER)
    c_tiled = c_full.reshape(ORDER, BTILES, TILE_B)
    alpha_tiles = alpha_values.reshape(PAIRS, ATILES, ANZ, ATILE, ATILE)
    alpha_lists = alpha_rows.reshape(PAIRS, ATILES, ANZ).astype(jnp.int32)

    def one_pair(summed, inputs):
        beta_tiles, beta_lists, pair_tiles, pair_lists = inputs
        picked = c_tiled[:, beta_lists].astype(jnp.float32)
        product = jnp.einsum("ajzt,jzts->ajs", picked, beta_tiles.astype(jnp.float32))
        rounded = lax.optimization_barrier(product.astype(jnp.bfloat16))
        x_matrix = rounded.astype(jnp.float32).reshape(ATILES, ATILE, ORDER)

        def one_slot(partial_value, slot):
            slot_tiles, slot_rows = slot
            contrib = jnp.einsum("quv,qvn->qun", slot_tiles.astype(jnp.float32), x_matrix)
            return partial_value.at[slot_rows].add(contrib), None

        summed, _ = lax.scan(one_slot, summed, (jnp.moveaxis(pair_tiles, 1, 0), jnp.moveaxis(pair_lists, 1, 0)))
        return summed, None

    start_sum = jnp.zeros((ATILES, ATILE, ORDER), jnp.float32)
    summed, _ = lax.scan(one_pair, start_sum, (beta_values, beta_rows.astype(jnp.int32), alpha_tiles, alpha_lists))
    y_matrix = summed.reshape(ORDER, ORDER)
    sigma = y_matrix + y_matrix.T
    return (sigma / gaps.reshape(ORDER, ORDER)).reshape(GROUPS, SPAN, ORDER)
```

```python
import functools

import jax
import jax.numpy as jnp
from jax import lax
from jax.experimental import pallas as pl
from jax.experimental.pallas import tpu as pltpu
from jax.sharding import PartitionSpec as P

CONTRACT_LAST = (((1,), (1,)), ((), ()))


def beta_kernel(listed, held, rows_ref, c_ref, b_ref, xt_ref):
    k, j = pl.program_id(0), pl.program_id(1)
    width = b_ref.shape[-1]
    picked = []
    for z in range(listed):
        tile = rows_ref[k, j, z]
        owner = tile // held
        start = pl.multiple_of((tile - owner * held) * width, width)
        picked.append(c_ref[owner, :, pl.ds(start, width)])
    lhs = b_ref[0, 0].reshape(listed * width, width)
    product = lax.dot_general(
        lhs, jnp.concatenate(picked, axis=1), (((0,), (1,)), ((), ())),
        preferred_element_type=jnp.float32,
    )
    xt_ref[0] = product.astype(xt_ref.dtype)


def beta_products(gathered, beta_values, beta_rows):
    pairs, tiles, listed, width, _ = beta_values.shape
    owners, rows, columns = gathered.shape
    return pl.pallas_call(
        functools.partial(beta_kernel, listed, columns // width),
        grid_spec=pltpu.PrefetchScalarGridSpec(
            num_scalar_prefetch=1,
            grid=(pairs, tiles),
            in_specs=[
                pl.BlockSpec((owners, rows, columns), lambda k, j, s: (0, 0, 0)),
                pl.BlockSpec((1, 1, listed, width, width), lambda k, j, s: (k, j, 0, 0, 0)),
            ],
            out_specs=pl.BlockSpec((1, width, rows), lambda k, j, s: (k, j, 0)),
        ),
        out_shape=jax.ShapeDtypeStruct((pairs, tiles * width, rows), jnp.bfloat16),
        compiler_params=pltpu.CompilerParams(vmem_limit_bytes=56 << 20),
        name="beta_products",
    )(beta_rows, gathered, beta_values)


def alpha_kernel(groups, rows_ref, a_ref, x_ref, own_ref, mirror_ref, acc_ref):
    r = pl.program_id(0)
    row_devices = pl.num_programs(0)
    pairs = x_ref.shape[1]
    listed, tile = a_ref.shape[2], a_ref.shape[3]

    @pl.when(r == 0)
    def _():
        acc_ref[...] = jnp.zeros_like(acc_ref)

    for k in range(pairs):
        for g in range(groups):
            x = x_ref[0, k, :, g * tile : (g + 1) * tile]
            slot = k * groups + g
            if tile % 16 == 0:
                product = lax.dot_general(
                    a_ref[0, slot].reshape(listed * tile, tile), x, CONTRACT_LAST,
                    preferred_element_type=jnp.float32,
                )
                for z in range(listed):
                    acc_ref[rows_ref[r, slot, z]] += product[z * tile : (z + 1) * tile]
            else:

                @pl.loop(0, listed)
                def _(z):
                    acc_ref[rows_ref[r, slot, z]] += lax.dot_general(
                        a_ref[0, slot, z], x, CONTRACT_LAST, preferred_element_type=jnp.float32
                    )

    @pl.when(r == row_devices - 1)
    def _():
        count = acc_ref.shape[0] // groups
        for g in range(groups):
            for to in range(count):
                turned = acc_ref[g * count + to].T.astype(own_ref.dtype)
                own_ref[to, :, g * tile : (g + 1) * tile] = turned
                mirror_ref[g, :, to * tile : (to + 1) * tile] = turned


def alpha_products(alpha_all, rows_all, x_strip, groups):
    row_devices, slots, listed, tile, _ = alpha_all.shape
    _, pairs, strip, _ = x_strip.shape
    return pl.pallas_call(
        functools.partial(alpha_kernel, groups),
        grid_spec=pltpu.PrefetchScalarGridSpec(
            num_scalar_prefetch=1,
            grid=(row_devices,),
            in_specs=[
                pl.BlockSpec((1, slots, listed, tile, tile), lambda r, s: (r, 0, 0, 0, 0)),
                pl.BlockSpec((1, pairs, strip, groups * tile), lambda r, s: (r, 0, 0, 0)),
            ],
            out_specs=[
                pl.BlockSpec((row_devices, strip, groups * tile), lambda r, s: (0, 0, 0)),
                pl.BlockSpec((groups, strip, row_devices * tile), lambda r, s: (0, 0, 0)),
            ],
            scratch_shapes=[pltpu.VMEM((groups * row_devices, tile, strip), jnp.float32)],
        ),
        out_shape=[
            jax.ShapeDtypeStruct((row_devices, strip, groups * tile), jnp.bfloat16),
            jax.ShapeDtypeStruct((groups, strip, row_devices * tile), jnp.bfloat16),
        ],
        compiler_params=pltpu.CompilerParams(vmem_limit_bytes=56 << 20),
        name="alpha_products",
    )(rows_all, alpha_all, x_strip)


def final_kernel(own_ref, mirror_ref, gaps_ref, out_ref):
    own = own_ref[...].astype(jnp.float32).T
    out_ref[...] = (own + mirror_ref[...].astype(jnp.float32)) / gaps_ref[...]


def final(own, mirror, gaps):
    rows, columns = gaps.shape
    block = next(n for n in (384, 256, 128) if columns % n == 0)
    wide = pl.BlockSpec((rows, block), lambda i: (0, i))
    return pl.pallas_call(
        final_kernel,
        grid=(columns // block,),
        in_specs=[pl.BlockSpec((block, rows), lambda i: (i, 0)), wide, wide],
        out_specs=wide,
        out_shape=jax.ShapeDtypeStruct((rows, columns), jnp.float32),
        name="final",
    )(own, mirror, gaps)


def per_device(c_matrix, beta_values, beta_rows, alpha_values, alpha_rows, gaps):
    row_devices = lax.axis_size("row")
    groups, stretch, columns = c_matrix.shape
    pairs, _, _, listed, tile, _ = alpha_values.shape
    rows_all = lax.all_gather(alpha_rows[:, :, 0].reshape(pairs * groups, listed), "row")
    gathered = lax.all_gather(c_matrix.reshape(groups * stretch, columns), "col")
    alpha_all = lax.all_gather(
        alpha_values[:, :, 0].reshape(pairs * groups, listed, tile, tile), "row"
    )
    xt = beta_products(gathered, beta_values, beta_rows)
    xt = jnp.moveaxis(xt.reshape(pairs, row_devices, stretch, groups * stretch), 1, 0)
    x_strip = lax.all_to_all(xt, "row", 0, 0)
    own, mirror = alpha_products(alpha_all, rows_all, x_strip, groups)
    own = lax.all_to_all(own, "row", 0, 0)
    mirror = lax.all_to_all(mirror, "col", 0, 0)
    out = final(
        own.reshape(columns, groups * stretch),
        mirror.reshape(groups * stretch, columns),
        gaps.reshape(groups * stretch, columns),
    )
    return out.reshape(gaps.shape)


def solution(mesh):
    placed = (
        P(None, "row", "col"),
        P(None, "col", None, None, None),
        P(None, "col", None),
        P(None, None, "row", None, None, None),
        P(None, None, "row", None),
        P(None, "row", "col"),
    )
    return jax.shard_map(
        per_device, mesh=mesh, in_specs=placed, out_specs=P(None, "row", "col"), check_vma=False
    )
```

```python
import functools

import jax
import jax.numpy as jnp
from jax import lax
from jax.experimental import pallas as pl
from jax.experimental.pallas import tpu as pltpu
from jax.sharding import PartitionSpec as P

CONTRACT_LAST = (((1,), (1,)), ((), ()))


def beta_kernel(listed, held, rows_ref, c_ref, b_ref, xt_ref):
    k, j = pl.program_id(0), pl.program_id(1)
    width = b_ref.shape[-1]
    picked = []
    for z in range(listed):
        tile = rows_ref[k, j, z]
        owner = tile // held
        start = pl.multiple_of((tile - owner * held) * width, width)
        picked.append(c_ref[owner, :, pl.ds(start, width)])
    lhs = b_ref[0, 0].reshape(listed * width, width)
    product = lax.dot_general(
        lhs, jnp.concatenate(picked, axis=1), (((0,), (1,)), ((), ())),
        preferred_element_type=jnp.float32,
    )
    xt_ref[0] = product.astype(xt_ref.dtype)


def beta_products(gathered, beta_values, beta_rows):
    pairs, tiles, listed, width, _ = beta_values.shape
    owners, rows, columns = gathered.shape
    return pl.pallas_call(
        functools.partial(beta_kernel, listed, columns // width),
        grid_spec=pltpu.PrefetchScalarGridSpec(
            num_scalar_prefetch=1,
            grid=(pairs, tiles),
            in_specs=[
                pl.BlockSpec((owners, rows, columns), lambda k, j, s: (0, 0, 0)),
                pl.BlockSpec((1, 1, listed, width, width), lambda k, j, s: (k, j, 0, 0, 0)),
            ],
            out_specs=pl.BlockSpec((1, width, rows), lambda k, j, s: (k, j, 0)),
        ),
        out_shape=jax.ShapeDtypeStruct((pairs, tiles * width, rows), jnp.bfloat16),
        compiler_params=pltpu.CompilerParams(vmem_limit_bytes=56 << 20),
        name="beta_products",
    )(beta_rows, gathered, beta_values)


def alpha_kernel(groups, rows_ref, a_ref, x_ref, own_ref, mirror_ref, acc_ref):
    r = pl.program_id(0)
    row_devices = pl.num_programs(0)
    pairs = x_ref.shape[2]
    listed, tile = a_ref.shape[2], a_ref.shape[3]

    @pl.when(r == 0)
    def _():
        acc_ref[...] = jnp.zeros_like(acc_ref)

    for k in range(pairs):
        parts = [x_ref[c, 0, k] for c in range(x_ref.shape[0])]
        merged = jnp.concatenate(parts, axis=1) if len(parts) > 1 else parts[0]
        for g in range(groups):
            x = merged[:, g * tile : (g + 1) * tile]
            slot = k * groups + g
            if tile % 16 == 0:
                product = lax.dot_general(
                    a_ref[0, slot].reshape(listed * tile, tile), x, CONTRACT_LAST,
                    preferred_element_type=jnp.float32,
                )
                for z in range(listed):
                    acc_ref[rows_ref[r, slot, z]] += product[z * tile : (z + 1) * tile]
            else:

                @pl.loop(0, listed)
                def _(z):
                    acc_ref[rows_ref[r, slot, z]] += lax.dot_general(
                        a_ref[0, slot, z], x, CONTRACT_LAST, preferred_element_type=jnp.float32
                    )

    @pl.when(r == row_devices - 1)
    def _():
        count = acc_ref.shape[0] // groups
        for g in range(groups):
            for to in range(count):
                turned = acc_ref[g * count + to].T.astype(own_ref.dtype)
                own_ref[to, :, g * tile : (g + 1) * tile] = turned
                mirror_ref[g, :, to * tile : (to + 1) * tile] = turned


def alpha_products(alpha_all, rows_all, x_strip, groups):
    row_devices, slots, listed, tile, _ = alpha_all.shape
    chunks, _, pairs, strip, chunk = x_strip.shape
    return pl.pallas_call(
        functools.partial(alpha_kernel, groups),
        grid_spec=pltpu.PrefetchScalarGridSpec(
            num_scalar_prefetch=1,
            grid=(row_devices,),
            in_specs=[
                pl.BlockSpec((1, slots, listed, tile, tile), lambda r, s: (r, 0, 0, 0, 0)),
                pl.BlockSpec((chunks, 1, pairs, strip, chunk), lambda r, s: (0, r, 0, 0, 0)),
            ],
            out_specs=[
                pl.BlockSpec((row_devices, strip, groups * tile), lambda r, s: (0, 0, 0)),
                pl.BlockSpec((groups, strip, row_devices * tile), lambda r, s: (0, 0, 0)),
            ],
            scratch_shapes=[pltpu.VMEM((groups * row_devices, tile, strip), jnp.float32)],
        ),
        out_shape=[
            jax.ShapeDtypeStruct((row_devices, strip, groups * tile), jnp.bfloat16),
            jax.ShapeDtypeStruct((groups, strip, row_devices * tile), jnp.bfloat16),
        ],
        compiler_params=pltpu.CompilerParams(vmem_limit_bytes=56 << 20),
        name="alpha_products",
    )(rows_all, alpha_all, x_strip)


def final_kernel(own_ref, mirror_ref, gaps_ref, out_ref):
    own = own_ref[...].astype(jnp.float32).T
    out_ref[...] = (own + mirror_ref[...].astype(jnp.float32)) / gaps_ref[...]


def final(own, mirror, gaps):
    rows, columns = gaps.shape
    block = next(n for n in (384, 256, 128) if columns % n == 0)
    wide = pl.BlockSpec((rows, block), lambda i: (0, i))
    return pl.pallas_call(
        final_kernel,
        grid=(columns // block,),
        in_specs=[pl.BlockSpec((block, rows), lambda i: (i, 0)), wide, wide],
        out_specs=wide,
        out_shape=jax.ShapeDtypeStruct((rows, columns), jnp.float32),
        name="final",
    )(own, mirror, gaps)


def greet(axes):
    barrier = pltpu.get_barrier_semaphore()
    total = 0
    for axis in axes:
        size, me = lax.axis_size(axis), lax.axis_index(axis)
        total += size - 1

        @pl.loop(1, size)
        def _(off):
            pl.semaphore_signal(
                barrier, inc=1, device_id={axis: lax.rem(me + off, size)},
                device_id_type=pl.DeviceIdType.MESH,
            )

    pl.semaphore_wait(barrier, total)


def remote(src, dst, send_sem, recv_sem, axis, peer):
    return pltpu.make_async_remote_copy(
        src_ref=src, dst_ref=dst, send_sem=send_sem, recv_sem=recv_sem,
        device_id={axis: peer}, device_id_type=pl.DeviceIdType.MESH,
    )


def spread_kernel(chunks, rows_ref, c_ref, b_ref, list_ref, x_ref, lists_ref, *scratch):
    held, sent = scratch[:chunks], scratch[chunks : 2 * chunks]
    local_sem, c_send, c_recv, x_send, x_recv, own_sem, l_send, l_recv, l_own = scratch[2 * chunks :]
    row_devices, row = lax.axis_size("row"), lax.axis_index("row")
    col_devices, col = lax.axis_size("col"), lax.axis_index("col")
    pairs, tiles, listed, width, _ = b_ref.shape
    per_owner, rows, _ = c_ref.shape
    chunk = rows // chunks
    strip = per_owner * width // row_devices

    def own_c(c):
        return pltpu.make_async_copy(
            c_ref.at[:, pl.ds(c * chunk, chunk)], held[c].at[pl.ds(col * per_owner, per_owner)],
            local_sem.at[c],
        )

    def send_c(c, off):
        return remote(
            c_ref.at[:, pl.ds(c * chunk, chunk)], held[c].at[pl.ds(col * per_owner, per_owner)],
            c_send.at[c, off - 1], c_recv.at[c, off - 1], "col", lax.rem(col + off, col_devices),
        )

    def send_x(c, off):
        peer = lax.rem(row + off, row_devices)
        start = pl.multiple_of(peer * strip, 16)
        return remote(
            sent[c].at[:, pl.ds(start, strip), :], x_ref.at[c, row], x_send.at[c, off - 1],
            x_recv.at[c, off - 1], "row", peer,
        )

    def own_x(c):
        start = pl.multiple_of(row * strip, 16)
        return pltpu.make_async_copy(
            sent[c].at[:, pl.ds(start, strip), :], x_ref.at[c, row], own_sem.at[c]
        )

    def send_list(off):
        return remote(
            list_ref, lists_ref.at[row], l_send.at[off - 1], l_recv.at[off - 1], "row",
            lax.rem(row + off, row_devices),
        )

    own_list = pltpu.make_async_copy(list_ref, lists_ref.at[row], l_own)
    for c in range(chunks):
        own_c(c).start()
    own_list.start()
    greet(("row", "col"))
    for c in range(chunks):
        for off in range(1, col_devices):
            send_c(c, off).start()

    @pl.loop(1, row_devices)
    def _(off):
        send_list(off).start()

    for c in range(chunks):
        own_c(c).wait()
        for off in range(1, col_devices):
            send_c(c, off).wait_recv()

        @pl.loop(0, tiles)
        def _(j):
            for k in range(pairs):
                picked = [held[c][rows_ref[k, j, z]] for z in range(listed)]
                product = lax.dot_general(
                    b_ref[k, j].reshape(listed * width, width), jnp.concatenate(picked, axis=1),
                    (((0,), (1,)), ((), ())), preferred_element_type=jnp.float32,
                )
                sent[c][k, pl.ds(pl.multiple_of(j * width, width), width), :] = product.astype(
                    jnp.bfloat16
                )

        @pl.loop(1, row_devices)
        def _(off):
            send_x(c, off).start()

        own_x(c).start()

    own_list.wait()

    @pl.loop(1, row_devices)
    def _(off):
        send_list(off).wait()

    for c in range(chunks):
        own_x(c).wait()
        for off in range(1, col_devices):
            send_c(c, off).wait_send()

        @pl.loop(1, row_devices)
        def _(off):
            send_x(c, off).wait()


def spread(c_matrix, beta_values, beta_rows, alpha_list, row_devices, col_devices, chunk):
    rows, columns = c_matrix.shape
    pairs, _, _, width, _ = beta_values.shape
    c_tiles = jnp.moveaxis(c_matrix.reshape(rows, columns // width, width), 1, 0)
    strip, chunks = columns // row_devices, rows // chunk
    dma = pltpu.SemaphoreType.DMA
    anywhere = pl.BlockSpec(memory_space=pl.ANY)
    return pl.pallas_call(
        functools.partial(spread_kernel, chunks),
        in_specs=[
            pl.BlockSpec(memory_space=pltpu.SMEM), anywhere,
            pl.BlockSpec(memory_space=pltpu.VMEM), pl.BlockSpec(memory_space=pltpu.VMEM),
        ],
        out_specs=[anywhere, anywhere],
        out_shape=[
            jax.ShapeDtypeStruct((chunks, row_devices, pairs, strip, chunk), jnp.bfloat16),
            jax.ShapeDtypeStruct((row_devices,) + alpha_list.shape, jnp.int32),
        ],
        scratch_shapes=[pltpu.VMEM((col_devices * columns // width, chunk, width), jnp.bfloat16)] * chunks
        + [pltpu.VMEM((pairs, columns, chunk), jnp.bfloat16)] * chunks
        + [
            dma((chunks,)), dma((chunks, col_devices - 1)), dma((chunks, col_devices - 1)),
            dma((chunks, row_devices - 1)), dma((chunks, row_devices - 1)), dma((chunks,)),
            dma((row_devices - 1,)), dma((row_devices - 1,)), dma,
        ],
        compiler_params=pltpu.CompilerParams(
            collective_id=0, has_side_effects=True, vmem_limit_bytes=56 << 20
        ),
        cost_estimate=pl.CostEstimate(
            flops=1 << 37, bytes_accessed=1 << 28, transcendentals=0
        ),
        name="spread",
    )(beta_rows, c_tiles, beta_values, alpha_list)


def exchange_kernel(own_ref, mirror_ref, own_out, mirror_out, o_send, o_recv, m_send, m_recv, sems):
    row_devices, row = lax.axis_size("row"), lax.axis_index("row")
    col_devices, col = lax.axis_size("col"), lax.axis_index("col")

    def send_own(off):
        peer = lax.rem(row + off, row_devices)
        return remote(
            own_ref.at[peer], own_out.at[row], o_send.at[off - 1], o_recv.at[off - 1], "row", peer
        )

    def send_mirror(off):
        peer = lax.rem(col + off, col_devices)
        return remote(
            mirror_ref.at[peer], mirror_out.at[col], m_send.at[off - 1], m_recv.at[off - 1],
            "col", peer,
        )

    stay_own = pltpu.make_async_copy(own_ref.at[row], own_out.at[row], sems.at[0])
    stay_mirror = pltpu.make_async_copy(mirror_ref.at[col], mirror_out.at[col], sems.at[1])
    greet(("row", "col"))

    @pl.loop(1, col_devices)
    def _(off):
        send_mirror(off).start()

    @pl.loop(1, row_devices)
    def _(off):
        send_own(off).start()

    stay_own.start()
    stay_mirror.start()
    stay_own.wait()
    stay_mirror.wait()

    @pl.loop(1, row_devices)
    def _(off):
        send_own(off).wait()

    @pl.loop(1, col_devices)
    def _(off):
        send_mirror(off).wait()


def exchange(own, mirror):
    dma = pltpu.SemaphoreType.DMA
    anywhere = pl.BlockSpec(memory_space=pl.ANY)
    local = pl.BlockSpec(memory_space=pltpu.VMEM)
    row_devices, col_devices = own.shape[0], mirror.shape[0]
    return pl.pallas_call(
        exchange_kernel,
        in_specs=[local, local],
        out_specs=[anywhere, anywhere],
        out_shape=[
            jax.ShapeDtypeStruct(own.shape, own.dtype),
            jax.ShapeDtypeStruct(mirror.shape, mirror.dtype),
        ],
        scratch_shapes=[
            dma((row_devices - 1,)), dma((row_devices - 1,)),
            dma((col_devices - 1,)), dma((col_devices - 1,)), dma((2,)),
        ],
        compiler_params=pltpu.CompilerParams(
            collective_id=1, has_side_effects=True, vmem_limit_bytes=56 << 20
        ),
        name="exchange",
    )(own, mirror)


def per_device(c_matrix, beta_values, beta_rows, alpha_values, alpha_rows, gaps):
    row_devices, col_devices = lax.axis_size("row"), lax.axis_size("col")
    groups, stretch, columns = c_matrix.shape
    pairs, _, _, listed, tile, _ = alpha_values.shape
    rows, chunk = groups * stretch, beta_values.shape[-1]
    c_rows = c_matrix.reshape(rows, columns)
    alpha_all = lax.all_gather(
        alpha_values[:, :, 0].reshape(pairs * groups, listed, tile, tile), "row"
    )
    alpha_list = alpha_rows[:, :, 0].reshape(pairs * groups, listed)
    own_kernels = stretch % 16 == 0 and rows % chunk == 0
    if own_kernels:
        entries = alpha_list.size
        padded = jnp.pad(alpha_list.reshape(-1), (0, -entries % 1024)).reshape(-1, 128)
        x_strip, rows_all = spread(
            c_rows, beta_values, beta_rows, padded, row_devices, col_devices, chunk
        )
        rows_all = rows_all.reshape(row_devices, -1)[:, :entries]
        rows_all = rows_all.reshape(row_devices, pairs * groups, listed)
    else:
        rows_all = lax.all_gather(alpha_list, "row")
        xt = beta_products(lax.all_gather(c_rows, "col"), beta_values, beta_rows)
        xt = jnp.moveaxis(xt.reshape(pairs, row_devices, stretch, rows), 1, 0)
        x_strip = lax.all_to_all(xt, "row", 0, 0)[None]
    own, mirror = alpha_products(alpha_all, rows_all, x_strip, groups)
    if own_kernels:
        own, mirror = exchange(own, mirror)
    else:
        own = lax.all_to_all(own, "row", 0, 0)
        mirror = lax.all_to_all(mirror, "col", 0, 0)
    out = final(
        own.reshape(columns, groups * stretch),
        mirror.reshape(groups * stretch, columns),
        gaps.reshape(groups * stretch, columns),
    )
    return out.reshape(gaps.shape)


def solution(mesh):
    placed = (
        P(None, "row", "col"),
        P(None, "col", None, None, None),
        P(None, "col", None),
        P(None, None, "row", None, None, None),
        P(None, None, "row", None),
        P(None, "row", "col"),
    )
    return jax.shard_map(
        per_device, mesh=mesh, in_specs=placed, out_specs=P(None, "row", "col"), check_vma=False
    )
```

```python
import functools

import jax
import jax.numpy as jnp
from jax import lax
from jax.experimental import pallas as pl
from jax.experimental.pallas import tpu as pltpu
from jax.sharding import PartitionSpec as P

CONTRACT_LAST = (((1,), (1,)), ((), ()))


def beta_kernel(listed, held, rows_ref, c_ref, b_ref, xt_ref):
    k, j = pl.program_id(0), pl.program_id(1)
    width = b_ref.shape[-1]
    picked = []
    for z in range(listed):
        tile = rows_ref[k, j, z]
        owner = tile // held
        start = pl.multiple_of((tile - owner * held) * width, width)
        picked.append(c_ref[owner, :, pl.ds(start, width)])
    lhs = b_ref[0, 0].reshape(listed * width, width)
    product = lax.dot_general(
        lhs, jnp.concatenate(picked, axis=1), (((0,), (1,)), ((), ())),
        preferred_element_type=jnp.float32,
    )
    xt_ref[0] = product.astype(xt_ref.dtype)


def beta_products(gathered, beta_values, beta_rows):
    pairs, tiles, listed, width, _ = beta_values.shape
    owners, rows, columns = gathered.shape
    return pl.pallas_call(
        functools.partial(beta_kernel, listed, columns // width),
        grid_spec=pltpu.PrefetchScalarGridSpec(
            num_scalar_prefetch=1,
            grid=(pairs, tiles),
            in_specs=[
                pl.BlockSpec((owners, rows, columns), lambda k, j, s: (0, 0, 0)),
                pl.BlockSpec((1, 1, listed, width, width), lambda k, j, s: (k, j, 0, 0, 0)),
            ],
            out_specs=pl.BlockSpec((1, width, rows), lambda k, j, s: (k, j, 0)),
        ),
        out_shape=jax.ShapeDtypeStruct((pairs, tiles * width, rows), jnp.bfloat16),
        compiler_params=pltpu.CompilerParams(vmem_limit_bytes=56 << 20),
        name="beta_products",
    )(beta_rows, gathered, beta_values)


def pack_alpha(tiles):
    count, listed, tile, _ = tiles.shape
    flat = tiles.reshape(count * listed * tile, tile)
    half, whole = flat.shape[0] // 2, tile // 128
    parts = [flat[:, i * 128 : (i + 1) * 128] for i in range(whole)]
    parts.append(jnp.concatenate([flat[:half, whole * 128 :], flat[half:, whole * 128 :]], axis=1))
    return jnp.concatenate(parts, axis=0)


def packed_product(a_ref, slot, slots, listed, tile, x):
    size, whole = listed * tile, tile // 128
    parts = [a_ref[0, pl.ds(i * slots * size + slot * size, size), :] for i in range(whole)]
    parts.append(a_ref[0, pl.ds(whole * slots * size + slot % (slots // 2) * size, size), :])
    blank = jnp.zeros((x.shape[0], 64), x.dtype)
    tail = [x[:, whole * 128 :], blank]
    if slot >= slots // 2:
        tail = tail[::-1]
    wide = jnp.concatenate([x[:, : whole * 128]] + tail, axis=1)
    return lax.dot_general(
        jnp.concatenate(parts, axis=1), wide, CONTRACT_LAST, preferred_element_type=jnp.float32
    )


def alpha_kernel(groups, rows_ref, a_ref, x_ref, own_ref, mirror_ref, acc_ref):
    r = pl.program_id(0)
    row_devices = pl.num_programs(0)
    pairs = x_ref.shape[2]
    listed, tile = rows_ref.shape[2], acc_ref.shape[1]

    @pl.when(r == 0)
    def _():
        acc_ref[...] = jnp.zeros_like(acc_ref)

    for k in range(pairs):
        parts = [x_ref[c, 0, k] for c in range(x_ref.shape[0])]
        merged = jnp.concatenate(parts, axis=1) if len(parts) > 1 else parts[0]
        for g in range(groups):
            x = merged[:, g * tile : (g + 1) * tile]
            slot = k * groups + g
            if len(a_ref.shape) == 3:
                product = packed_product(a_ref, slot, pairs * groups, listed, tile, x)
                for z in range(listed):
                    acc_ref[rows_ref[r, slot, z]] += product[z * tile : (z + 1) * tile]
            else:

                @pl.loop(0, listed)
                def _(z):
                    acc_ref[rows_ref[r, slot, z]] += lax.dot_general(
                        a_ref[0, slot, z], x, CONTRACT_LAST, preferred_element_type=jnp.float32
                    )

    @pl.when(r == row_devices - 1)
    def _():
        count = acc_ref.shape[0] // groups
        for g in range(groups):
            for to in range(count):
                turned = acc_ref[g * count + to].T.astype(own_ref.dtype)
                own_ref[to, :, g * tile : (g + 1) * tile] = turned
                mirror_ref[g, :, to * tile : (to + 1) * tile] = turned


def alpha_products(alpha_all, rows_all, x_strip, groups):
    row_devices, rest = alpha_all.shape[0], alpha_all.shape[1:]
    tile = x_strip.shape[0] * x_strip.shape[-1] // groups
    chunks, _, pairs, strip, chunk = x_strip.shape
    return pl.pallas_call(
        functools.partial(alpha_kernel, groups),
        grid_spec=pltpu.PrefetchScalarGridSpec(
            num_scalar_prefetch=1,
            grid=(row_devices,),
            in_specs=[
                pl.BlockSpec((1,) + rest, lambda r, s: (r,) + (0,) * len(rest)),
                pl.BlockSpec((chunks, 1, pairs, strip, chunk), lambda r, s: (0, r, 0, 0, 0)),
            ],
            out_specs=[
                pl.BlockSpec((row_devices, strip, groups * tile), lambda r, s: (0, 0, 0)),
                pl.BlockSpec((groups, strip, row_devices * tile), lambda r, s: (0, 0, 0)),
            ],
            scratch_shapes=[pltpu.VMEM((groups * row_devices, tile, strip), jnp.float32)],
        ),
        out_shape=[
            jax.ShapeDtypeStruct((row_devices, strip, groups * tile), jnp.bfloat16),
            jax.ShapeDtypeStruct((groups, strip, row_devices * tile), jnp.bfloat16),
        ],
        compiler_params=pltpu.CompilerParams(vmem_limit_bytes=56 << 20),
        name="alpha_products",
    )(rows_all, alpha_all, x_strip)


def final_kernel(own_ref, mirror_ref, gaps_ref, out_ref):
    own = own_ref[...].astype(jnp.float32).T
    out_ref[...] = (own + mirror_ref[...].astype(jnp.float32)) / gaps_ref[...]


def final(own, mirror, gaps):
    rows, columns = gaps.shape
    block = next(n for n in (384, 256, 128) if columns % n == 0)
    wide = pl.BlockSpec((rows, block), lambda i: (0, i))
    return pl.pallas_call(
        final_kernel,
        grid=(columns // block,),
        in_specs=[pl.BlockSpec((block, rows), lambda i: (i, 0)), wide, wide],
        out_specs=wide,
        out_shape=jax.ShapeDtypeStruct((rows, columns), jnp.float32),
        name="final",
    )(own, mirror, gaps)


def greet(axes):
    barrier = pltpu.get_barrier_semaphore()
    total = 0
    for axis in axes:
        size, me = lax.axis_size(axis), lax.axis_index(axis)
        total += size - 1

        @pl.loop(1, size)
        def _(off):
            pl.semaphore_signal(
                barrier, inc=1, device_id={axis: lax.rem(me + off, size)},
                device_id_type=pl.DeviceIdType.MESH,
            )

    pl.semaphore_wait(barrier, total)


def remote(src, dst, send_sem, recv_sem, axis, peer):
    return pltpu.make_async_remote_copy(
        src_ref=src, dst_ref=dst, send_sem=send_sem, recv_sem=recv_sem,
        device_id={axis: peer}, device_id_type=pl.DeviceIdType.MESH,
    )


def spread_kernel(chunks, rows_ref, c_ref, b_ref, list_ref, a_ref, x_ref, lists_ref, all_ref, *scratch):
    held, sent = scratch[:chunks], scratch[chunks : 2 * chunks]
    (local_sem, c_send, c_recv, x_send, x_recv, own_sem, l_send, l_recv, l_own, up_send, up_recv,
     down_send, down_recv, y_send, y_recv, core_send, core_recv, a_own) = scratch[2 * chunks :]
    row_devices, row = lax.axis_size("row"), lax.axis_index("row")
    col_devices, col = lax.axis_size("col"), lax.axis_index("col")
    pairs, tiles, listed, width, _ = b_ref.shape
    per_owner, rows, _ = c_ref.shape
    chunk = rows // chunks
    strip = per_owner * width // row_devices

    def own_c(c):
        return pltpu.make_async_copy(
            c_ref.at[:, pl.ds(c * chunk, chunk)], held[c].at[pl.ds(col * per_owner, per_owner)],
            local_sem.at[c],
        )

    def send_c(c, off):
        return remote(
            c_ref.at[:, pl.ds(c * chunk, chunk)], held[c].at[pl.ds(col * per_owner, per_owner)],
            c_send.at[c, off - 1], c_recv.at[c, off - 1], "col", lax.rem(col + off, col_devices),
        )

    def send_x(c, off):
        peer = lax.rem(row + off, row_devices)
        start = pl.multiple_of(peer * strip, 16)
        return remote(
            sent[c].at[:, pl.ds(start, strip), :], x_ref.at[c, row], x_send.at[c, off - 1],
            x_recv.at[c, off - 1], "row", peer,
        )

    def own_x(c):
        start = pl.multiple_of(row * strip, 16)
        return pltpu.make_async_copy(
            sent[c].at[:, pl.ds(start, strip), :], x_ref.at[c, row], own_sem.at[c]
        )

    def send_list(off):
        return remote(
            list_ref, lists_ref.at[row], l_send.at[off - 1], l_recv.at[off - 1], "row",
            lax.rem(row + off, row_devices),
        )

    lines = row_devices // 4
    z, y, core = row // 4, lax.rem(row // 2, 2), lax.rem(row, 2)

    def block(at_z, at_y, at_core):
        return (at_z * 2 + at_y) * 2 + at_core

    def hand(source, at, send_sem, recv_sem, peer):
        return remote(source, all_ref.at[at], send_sem, recv_sem, "row", peer)

    def up(step, first=False):
        at = block(z - step, y, core)
        source = a_ref if first else all_ref.at[at]
        return hand(source, at, up_send.at[step], up_recv.at[step], block(z + 1, y, core))

    def down(step, first=False):
        at = block(z + step, y, core)
        source = a_ref if first else all_ref.at[at]
        return hand(source, at, down_send.at[step], down_recv.at[step], block(z - 1, y, core))

    def over_y(at_z, first=False):
        at = block(at_z, y, core)
        source = a_ref if first else all_ref.at[at]
        return hand(source, at, y_send.at[at_z], y_recv.at[at_z], block(z, 1 - y, core))

    def over_core(at_z, at_y, first=False):
        at = block(at_z, at_y, core)
        source = a_ref if first else all_ref.at[at]
        sem = at_z * 2 + at_y
        return hand(source, at, core_send.at[sem], core_recv.at[sem], block(z, y, 1 - core))

    def arrived(at, recv_sem, send_sem):
        hand(all_ref.at[at], at, send_sem, recv_sem, block(z, y, 1 - core)).wait_recv()

    def relay(step):
        @pl.when(z - 1 - step >= 0)
        def _():
            arrived(block(z - 1 - step, y, core), up_recv.at[step], up_send.at[step])
            if step + 1 < lines - 1:

                @pl.when(z + 1 < lines)
                def _():
                    up(step + 1).start()

            over_y(z - 1 - step).start()
            over_core(z - 1 - step, y).start()

        @pl.when(z + 1 + step < lines)
        def _():
            arrived(block(z + 1 + step, y, core), down_recv.at[step], down_send.at[step])
            if step + 1 < lines - 1:

                @pl.when(z >= 1)
                def _():
                    down(step + 1).start()

            over_y(z + 1 + step).start()
            over_core(z + 1 + step, y).start()

    def cross(step):
        at_z = lax.rem(z + step, lines)
        arrived(block(at_z, 1 - y, core), y_recv.at[at_z], y_send.at[at_z])
        over_core(at_z, 1 - y).start()

    own_a = pltpu.make_async_copy(a_ref, all_ref.at[row], a_own)
    own_list = pltpu.make_async_copy(list_ref, lists_ref.at[row], l_own)
    for c in range(chunks):
        own_c(c).start()
    own_list.start()
    own_a.start()
    greet(("row", "col"))
    for c in range(chunks):
        for off in range(1, col_devices):
            send_c(c, off).start()

    @pl.when(z + 1 < lines)
    def _():
        up(0, True).start()

    @pl.when(z >= 1)
    def _():
        down(0, True).start()

    over_y(z, True).start()
    over_core(z, y, True).start()

    @pl.loop(1, row_devices)
    def _(off):
        send_list(off).start()

    relayed = 0
    for c in range(chunks):
        if relayed < lines - 1:
            relay(relayed)
            relayed += 1
        own_c(c).wait()
        for off in range(1, col_devices):
            send_c(c, off).wait_recv()

        @pl.loop(0, tiles)
        def _(j):
            for k in range(pairs):
                picked = [held[c][rows_ref[k, j, z]] for z in range(listed)]
                product = lax.dot_general(
                    b_ref[k, j].reshape(listed * width, width), jnp.concatenate(picked, axis=1),
                    (((0,), (1,)), ((), ())), preferred_element_type=jnp.float32,
                )
                sent[c][k, pl.ds(pl.multiple_of(j * width, width), width), :] = product.astype(
                    jnp.bfloat16
                )

        @pl.loop(1, row_devices)
        def _(off):
            send_x(c, off).start()

        own_x(c).start()
        if c == 0:
            cross(0)

    for step in range(relayed, lines - 1):
        relay(step)
    for step in range(1, lines):
        cross(step)
    own_a.wait()
    for step in range(lines - 1):

        @pl.when((z - step >= 0) & (z + 1 < lines))
        def _():
            up(step, step == 0).wait_send()

        @pl.when((z + step < lines) & (z >= 1))
        def _():
            down(step, step == 0).wait_send()

    for at_z in range(lines):
        over_y(at_z).wait_send()
        for at_y in range(2):
            over_core(at_z, at_y).wait_send()
            sem = at_z * 2 + at_y
            arrived(block(at_z, at_y, 1 - core), core_recv.at[sem], core_send.at[sem])
    own_list.wait()

    @pl.loop(1, row_devices)
    def _(off):
        send_list(off).wait()

    for c in range(chunks):
        own_x(c).wait()
        for off in range(1, col_devices):
            send_c(c, off).wait_send()

        @pl.loop(1, row_devices)
        def _(off):
            send_x(c, off).wait()


def spread(c_matrix, beta_values, beta_rows, alpha_list, packed, row_devices, col_devices, chunk):
    rows, columns = c_matrix.shape
    pairs, _, _, width, _ = beta_values.shape
    c_tiles = jnp.moveaxis(c_matrix.reshape(rows, columns // width, width), 1, 0)
    strip, chunks = columns // row_devices, rows // chunk
    dma = pltpu.SemaphoreType.DMA
    anywhere = pl.BlockSpec(memory_space=pl.ANY)
    return pl.pallas_call(
        functools.partial(spread_kernel, chunks),
        in_specs=[
            pl.BlockSpec(memory_space=pltpu.SMEM), anywhere,
            pl.BlockSpec(memory_space=pltpu.VMEM), pl.BlockSpec(memory_space=pltpu.VMEM),
            pl.BlockSpec(memory_space=pltpu.VMEM),
        ],
        out_specs=[anywhere, anywhere, anywhere],
        out_shape=[
            jax.ShapeDtypeStruct((chunks, row_devices, pairs, strip, chunk), jnp.bfloat16),
            jax.ShapeDtypeStruct((row_devices,) + alpha_list.shape, jnp.int32),
            jax.ShapeDtypeStruct((row_devices,) + packed.shape, packed.dtype),
        ],
        scratch_shapes=[pltpu.VMEM((col_devices * columns // width, chunk, width), jnp.bfloat16)] * chunks
        + [pltpu.VMEM((pairs, columns, chunk), jnp.bfloat16)] * chunks
        + [
            dma((chunks,)), dma((chunks, col_devices - 1)), dma((chunks, col_devices - 1)),
            dma((chunks, row_devices - 1)), dma((chunks, row_devices - 1)), dma((chunks,)),
            dma((row_devices - 1,)), dma((row_devices - 1,)), dma,
        ]
        + [dma((row_devices // 4 - 1,))] * 4
        + [dma((row_devices // 4,))] * 2
        + [dma((row_devices // 2,))] * 2
        + [dma],
        compiler_params=pltpu.CompilerParams(
            collective_id=0, has_side_effects=True, vmem_limit_bytes=56 << 20
        ),
        cost_estimate=pl.CostEstimate(
            flops=1 << 37, bytes_accessed=1 << 28, transcendentals=0
        ),
        name="spread",
    )(beta_rows, c_tiles, beta_values, alpha_list, packed)


def exchange_kernel(own_ref, mirror_ref, own_out, mirror_out, o_send, o_recv, m_send, m_recv, sems):
    row_devices, row = lax.axis_size("row"), lax.axis_index("row")
    col_devices, col = lax.axis_size("col"), lax.axis_index("col")

    def send_own(off):
        peer = lax.rem(row + off, row_devices)
        return remote(
            own_ref.at[peer], own_out.at[row], o_send.at[off - 1], o_recv.at[off - 1], "row", peer
        )

    def send_mirror(off):
        peer = lax.rem(col + off, col_devices)
        return remote(
            mirror_ref.at[peer], mirror_out.at[col], m_send.at[off - 1], m_recv.at[off - 1],
            "col", peer,
        )

    stay_own = pltpu.make_async_copy(own_ref.at[row], own_out.at[row], sems.at[0])
    stay_mirror = pltpu.make_async_copy(mirror_ref.at[col], mirror_out.at[col], sems.at[1])
    greet(("row", "col"))

    @pl.loop(1, col_devices)
    def _(off):
        send_mirror(off).start()

    @pl.loop(1, row_devices)
    def _(off):
        send_own(off).start()

    stay_own.start()
    stay_mirror.start()
    stay_own.wait()
    stay_mirror.wait()

    @pl.loop(1, row_devices)
    def _(off):
        send_own(off).wait()

    @pl.loop(1, col_devices)
    def _(off):
        send_mirror(off).wait()


def exchange(own, mirror):
    dma = pltpu.SemaphoreType.DMA
    anywhere = pl.BlockSpec(memory_space=pl.ANY)
    local = pl.BlockSpec(memory_space=pltpu.VMEM)
    row_devices, col_devices = own.shape[0], mirror.shape[0]
    return pl.pallas_call(
        exchange_kernel,
        in_specs=[local, local],
        out_specs=[anywhere, anywhere],
        out_shape=[
            jax.ShapeDtypeStruct(own.shape, own.dtype),
            jax.ShapeDtypeStruct(mirror.shape, mirror.dtype),
        ],
        scratch_shapes=[
            dma((row_devices - 1,)), dma((row_devices - 1,)),
            dma((col_devices - 1,)), dma((col_devices - 1,)), dma((2,)),
        ],
        compiler_params=pltpu.CompilerParams(
            collective_id=1, has_side_effects=True, vmem_limit_bytes=56 << 20
        ),
        name="exchange",
    )(own, mirror)


def per_device(c_matrix, beta_values, beta_rows, alpha_values, alpha_rows, gaps):
    row_devices, col_devices = lax.axis_size("row"), lax.axis_size("col")
    groups, stretch, columns = c_matrix.shape
    pairs, _, _, listed, tile, _ = alpha_values.shape
    rows, chunk = groups * stretch, beta_values.shape[-1]
    c_rows = c_matrix.reshape(rows, columns)
    alpha_tiles = alpha_values[:, :, 0].reshape(pairs * groups, listed, tile, tile)
    alpha_list = alpha_rows[:, :, 0].reshape(pairs * groups, listed)
    own_kernels = stretch % 16 == 0 and rows % chunk == 0 and tile % 128 == 64
    own_kernels = own_kernels and row_devices % 4 == 0 and pairs * groups % 2 == 0
    if own_kernels:
        entries = alpha_list.size
        padded = jnp.pad(alpha_list.reshape(-1), (0, -entries % 1024)).reshape(-1, 128)
        x_strip, rows_all, alpha_all = spread(
            c_rows, beta_values, beta_rows, padded, pack_alpha(alpha_tiles), row_devices,
            col_devices, chunk,
        )
        rows_all = rows_all.reshape(row_devices, -1)[:, :entries]
        rows_all = rows_all.reshape(row_devices, pairs * groups, listed)
    else:
        rows_all = lax.all_gather(alpha_list, "row")
        alpha_all = lax.all_gather(alpha_tiles, "row")
        xt = beta_products(lax.all_gather(c_rows, "col"), beta_values, beta_rows)
        xt = jnp.moveaxis(xt.reshape(pairs, row_devices, stretch, rows), 1, 0)
        x_strip = lax.all_to_all(xt, "row", 0, 0)[None]
    own, mirror = alpha_products(alpha_all, rows_all, x_strip, groups)
    if own_kernels:
        own, mirror = exchange(own, mirror)
    else:
        own = lax.all_to_all(own, "row", 0, 0)
        mirror = lax.all_to_all(mirror, "col", 0, 0)
    out = final(
        own.reshape(columns, groups * stretch),
        mirror.reshape(groups * stretch, columns),
        gaps.reshape(groups * stretch, columns),
    )
    return out.reshape(gaps.shape)


def solution(mesh):
    placed = (
        P(None, "row", "col"),
        P(None, "col", None, None, None),
        P(None, "col", None),
        P(None, None, "row", None, None, None),
        P(None, None, "row", None),
        P(None, "row", "col"),
    )
    return jax.shard_map(
        per_device, mesh=mesh, in_specs=placed, out_specs=P(None, "row", "col"), check_vma=False
    )
```

```python
import functools

import jax
import jax.numpy as jnp
from jax import lax
from jax.experimental import pallas as pl
from jax.experimental.pallas import tpu as pltpu
from jax.sharding import PartitionSpec as P

CONTRACT_LAST = (((1,), (1,)), ((), ()))


def beta_kernel(listed, held, rows_ref, c_ref, b_ref, xt_ref):
    k, j = pl.program_id(0), pl.program_id(1)
    width = b_ref.shape[-1]
    picked = []
    for z in range(listed):
        tile = rows_ref[k, j, z]
        owner = tile // held
        start = pl.multiple_of((tile - owner * held) * width, width)
        picked.append(c_ref[owner, :, pl.ds(start, width)])
    lhs = b_ref[0, 0].reshape(listed * width, width)
    product = lax.dot_general(
        lhs, jnp.concatenate(picked, axis=1), (((0,), (1,)), ((), ())),
        preferred_element_type=jnp.float32,
    )
    xt_ref[0] = product.astype(xt_ref.dtype)


def beta_products(gathered, beta_values, beta_rows):
    pairs, tiles, listed, width, _ = beta_values.shape
    owners, rows, columns = gathered.shape
    return pl.pallas_call(
        functools.partial(beta_kernel, listed, columns // width),
        grid_spec=pltpu.PrefetchScalarGridSpec(
            num_scalar_prefetch=1,
            grid=(pairs, tiles),
            in_specs=[
                pl.BlockSpec((owners, rows, columns), lambda k, j, s: (0, 0, 0)),
                pl.BlockSpec((1, 1, listed, width, width), lambda k, j, s: (k, j, 0, 0, 0)),
            ],
            out_specs=pl.BlockSpec((1, width, rows), lambda k, j, s: (k, j, 0)),
        ),
        out_shape=jax.ShapeDtypeStruct((pairs, tiles * width, rows), jnp.bfloat16),
        compiler_params=pltpu.CompilerParams(vmem_limit_bytes=56 << 20),
        name="beta_products",
    )(beta_rows, gathered, beta_values)


def pack_alpha(flat_ref, packed_ref):
    size, tile = flat_ref.shape
    half, whole = size // 2, tile // 128
    for i in range(whole):
        packed_ref[pl.ds(i * size, size), :] = flat_ref[:, i * 128 : (i + 1) * 128]
    packed_ref[pl.ds(whole * size, half), :] = jnp.concatenate(
        [flat_ref[pl.ds(0, half), whole * 128 :], flat_ref[pl.ds(half, half), whole * 128 :]], axis=1
    )


def packed_product(a_ref, at, slot, slots, listed, tile, x):
    size, whole = listed * tile, tile // 128
    parts = [a_ref[at, pl.ds(i * slots * size + slot * size, size), :] for i in range(whole)]
    parts.append(a_ref[at, pl.ds(whole * slots * size + slot % (slots // 2) * size, size), :])
    blank = jnp.zeros((x.shape[0], 64), x.dtype)
    tail = [x[:, whole * 128 :], blank]
    if slot >= slots // 2:
        tail = tail[::-1]
    wide = jnp.concatenate([x[:, : whole * 128]] + tail, axis=1)
    return lax.dot_general(
        jnp.concatenate(parts, axis=1), wide, CONTRACT_LAST, preferred_element_type=jnp.float32
    )


def alpha_kernel(groups, rows_ref, a_ref, x_ref, own_ref, mirror_ref, acc_ref):
    r = pl.program_id(0)
    row_devices = pl.num_programs(0)
    pairs = x_ref.shape[2]
    listed, tile = rows_ref.shape[2], acc_ref.shape[1]

    @pl.when(r == 0)
    def _():
        acc_ref[...] = jnp.zeros_like(acc_ref)

    for i in range(x_ref.shape[1]):
        at = r * x_ref.shape[1] + i
        for k in range(pairs):
            parts = [x_ref[c, i, k] for c in range(x_ref.shape[0])]
            merged = jnp.concatenate(parts, axis=1) if len(parts) > 1 else parts[0]
            for g in range(groups):
                x = merged[:, g * tile : (g + 1) * tile]
                slot = k * groups + g
                if len(a_ref.shape) == 3:
                    product = packed_product(a_ref, i, slot, pairs * groups, listed, tile, x)
                    for z in range(listed):
                        acc_ref[rows_ref[at, slot, z]] += product[z * tile : (z + 1) * tile]
                else:

                    @pl.loop(0, listed)
                    def _(z):
                        acc_ref[rows_ref[at, slot, z]] += lax.dot_general(
                            a_ref[i, slot, z], x, CONTRACT_LAST,
                            preferred_element_type=jnp.float32,
                        )

    @pl.when(r == row_devices - 1)
    def _():
        count = acc_ref.shape[0] // groups
        for g in range(groups):
            for to in range(count):
                turned = acc_ref[g * count + to].astype(own_ref.dtype).T
                own_ref[to, :, g * tile : (g + 1) * tile] = turned
                mirror_ref[g, :, to * tile : (to + 1) * tile] = turned


def alpha_products(alpha_all, rows_all, x_strip, groups):
    row_devices, rest = alpha_all.shape[0], alpha_all.shape[1:]
    tile = x_strip.shape[0] * x_strip.shape[-1] // groups
    per = 2 if len(rest) == 2 and row_devices % 2 == 0 else 1
    chunks, _, pairs, strip, chunk = x_strip.shape
    return pl.pallas_call(
        functools.partial(alpha_kernel, groups),
        grid_spec=pltpu.PrefetchScalarGridSpec(
            num_scalar_prefetch=1,
            grid=(row_devices // per,),
            in_specs=[
                pl.BlockSpec((per,) + rest, lambda r, s: (r,) + (0,) * len(rest)),
                pl.BlockSpec((chunks, per, pairs, strip, chunk), lambda r, s: (0, r, 0, 0, 0)),
            ],
            out_specs=[
                pl.BlockSpec((row_devices, strip, groups * tile), lambda r, s: (0, 0, 0)),
                pl.BlockSpec((groups, strip, row_devices * tile), lambda r, s: (0, 0, 0)),
            ],
            scratch_shapes=[pltpu.VMEM((groups * row_devices, tile, strip), jnp.float32)],
        ),
        out_shape=[
            jax.ShapeDtypeStruct((row_devices, strip, groups * tile), jnp.bfloat16),
            jax.ShapeDtypeStruct((groups, strip, row_devices * tile), jnp.bfloat16),
        ],
        compiler_params=pltpu.CompilerParams(vmem_limit_bytes=56 << 20),
        name="alpha_products",
    )(rows_all, alpha_all, x_strip)


def final_kernel(own_ref, mirror_ref, gaps_ref, out_ref):
    own = own_ref[...].T.astype(jnp.float32)
    out_ref[...] = (own + mirror_ref[...].astype(jnp.float32)) / gaps_ref[...]


def final(own, mirror, gaps):
    rows, columns = gaps.shape
    block = next(n for n in (384, 256, 128) if columns % n == 0)
    wide = pl.BlockSpec((rows, block), lambda i: (0, i))
    return pl.pallas_call(
        final_kernel,
        grid=(columns // block,),
        in_specs=[pl.BlockSpec((block, rows), lambda i: (i, 0)), wide, wide],
        out_specs=wide,
        out_shape=jax.ShapeDtypeStruct((rows, columns), jnp.float32),
        name="final",
    )(own, mirror, gaps)


def greet(axes):
    barrier = pltpu.get_barrier_semaphore()
    total = 0
    for axis in axes:
        size, me = lax.axis_size(axis), lax.axis_index(axis)
        total += size - 1

        @pl.loop(1, size)
        def _(off):
            pl.semaphore_signal(
                barrier, inc=1, device_id={axis: lax.rem(me + off, size)},
                device_id_type=pl.DeviceIdType.MESH,
            )

    pl.semaphore_wait(barrier, total)


def remote(src, dst, send_sem, recv_sem, axis, peer):
    return pltpu.make_async_remote_copy(
        src_ref=src, dst_ref=dst, send_sem=send_sem, recv_sem=recv_sem,
        device_id={axis: peer}, device_id_type=pl.DeviceIdType.MESH,
    )


def spread_kernel(chunks, rows_ref, c_ref, b_ref, list_ref, flat_ref, x_ref, lists_ref, all_ref, *scratch):
    held, sent = scratch[:chunks], scratch[chunks : 2 * chunks]
    (local_sem, c_send, c_recv, x_send, x_recv, own_sem, l_send, l_recv, l_own, up_send, up_recv,
     down_send, down_recv, y_send, y_recv, core_send, core_recv, a_own, a_ref) = scratch[2 * chunks :]
    row_devices, row = lax.axis_size("row"), lax.axis_index("row")
    col_devices, col = lax.axis_size("col"), lax.axis_index("col")
    pairs, tiles, listed, width, _ = b_ref.shape
    rows, columns = c_ref.shape
    per_owner = columns // width
    chunk = rows // chunks
    strip = per_owner * width // row_devices

    def own_c(c, t):
        return pltpu.make_async_copy(
            c_ref.at[pl.ds(c * chunk, chunk), pl.ds(pl.multiple_of(t * width, width), width)],
            held[c].at[col * per_owner + t], local_sem.at[c, t],
        )

    def send_c(c, off, t):
        return remote(
            c_ref.at[pl.ds(c * chunk, chunk), pl.ds(pl.multiple_of(t * width, width), width)],
            held[c].at[col * per_owner + t], c_send.at[c, off - 1, t], c_recv.at[c, off - 1, t],
            "col", lax.rem(col + off, col_devices),
        )

    def send_x(c, off):
        peer = lax.rem(row + off, row_devices)
        start = pl.multiple_of(peer * strip, 16)
        return remote(
            sent[c].at[:, pl.ds(start, strip), :], x_ref.at[c, row], x_send.at[c, off - 1],
            x_recv.at[c, off - 1], "row", peer,
        )

    def own_x(c):
        start = pl.multiple_of(row * strip, 16)
        return pltpu.make_async_copy(
            sent[c].at[:, pl.ds(start, strip), :], x_ref.at[c, row], own_sem.at[c]
        )

    def send_list(off):
        return remote(
            list_ref, lists_ref.at[row], l_send.at[off - 1], l_recv.at[off - 1], "row",
            lax.rem(row + off, row_devices),
        )

    lines = row_devices // 4
    z, y, core = row // 4, lax.rem(row // 2, 2), lax.rem(row, 2)

    def block(at_z, at_y, at_core):
        return (at_z * 2 + at_y) * 2 + at_core

    def hand(source, at, send_sem, recv_sem, peer):
        return remote(source, all_ref.at[at], send_sem, recv_sem, "row", peer)

    def up(step, first=False):
        at = block(z - step, y, core)
        source = a_ref if first else all_ref.at[at]
        return hand(source, at, up_send.at[step], up_recv.at[step], block(z + 1, y, core))

    def down(step, first=False):
        at = block(z + step, y, core)
        source = a_ref if first else all_ref.at[at]
        return hand(source, at, down_send.at[step], down_recv.at[step], block(z - 1, y, core))

    def over_y(at_z, first=False):
        at = block(at_z, y, core)
        source = a_ref if first else all_ref.at[at]
        return hand(source, at, y_send.at[at_z], y_recv.at[at_z], block(z, 1 - y, core))

    def over_core(at_z, at_y, first=False):
        at = block(at_z, at_y, core)
        source = a_ref if first else all_ref.at[at]
        sem = at_z * 2 + at_y
        return hand(source, at, core_send.at[sem], core_recv.at[sem], block(z, y, 1 - core))

    def arrived(at, recv_sem, send_sem):
        hand(all_ref.at[at], at, send_sem, recv_sem, block(z, y, 1 - core)).wait_recv()

    def relay(step):
        @pl.when(z - 1 - step >= 0)
        def _():
            arrived(block(z - 1 - step, y, core), up_recv.at[step], up_send.at[step])
            if step + 1 < lines - 1:

                @pl.when(z + 1 < lines)
                def _():
                    up(step + 1).start()

            over_y(z - 1 - step).start()
            over_core(z - 1 - step, y).start()

        @pl.when(z + 1 + step < lines)
        def _():
            arrived(block(z + 1 + step, y, core), down_recv.at[step], down_send.at[step])
            if step + 1 < lines - 1:

                @pl.when(z >= 1)
                def _():
                    down(step + 1).start()

            over_y(z + 1 + step).start()
            over_core(z + 1 + step, y).start()

    def cross(step):
        at_z = lax.rem(z + step, lines)
        arrived(block(at_z, 1 - y, core), y_recv.at[at_z], y_send.at[at_z])
        over_core(at_z, 1 - y).start()

    own_a = pltpu.make_async_copy(a_ref, all_ref.at[row], a_own)
    own_list = pltpu.make_async_copy(list_ref, lists_ref.at[row], l_own)
    for c in range(chunks):

        @pl.loop(0, per_owner)
        def _(t):
            own_c(c, t).start()

    own_list.start()
    pack_alpha(flat_ref, a_ref)
    greet(("row", "col"))
    for c in range(chunks):
        for off in range(1, col_devices):

            @pl.loop(0, per_owner)
            def _(t):
                send_c(c, off, t).start()

    @pl.when(z + 1 < lines)
    def _():
        up(0, True).start()

    @pl.when(z >= 1)
    def _():
        down(0, True).start()

    over_y(z, True).start()
    over_core(z, y, True).start()
    own_a.start()

    @pl.loop(1, row_devices)
    def _(off):
        send_list(off).start()

    relayed = 0
    for c in range(chunks):
        if relayed < lines - 1:
            relay(relayed)
            relayed += 1

        @pl.loop(0, per_owner)
        def _(t):
            own_c(c, t).wait()
            for off in range(1, col_devices):
                send_c(c, off, t).wait_recv()

        @pl.loop(0, tiles)
        def _(j):
            for k in range(pairs):
                picked = [held[c][rows_ref[k, j, z]] for z in range(listed)]
                product = lax.dot_general(
                    b_ref[k, j].reshape(listed * width, width), jnp.concatenate(picked, axis=1),
                    (((0,), (1,)), ((), ())), preferred_element_type=jnp.float32,
                )
                sent[c][k, pl.ds(pl.multiple_of(j * width, width), width), :] = product.astype(
                    jnp.bfloat16
                )

        @pl.loop(1, row_devices)
        def _(off):
            send_x(c, off).start()

        own_x(c).start()
        if c == 0:
            cross(0)

    for step in range(relayed, lines - 1):
        relay(step)
    for step in range(1, lines):
        cross(step)
    own_a.wait()
    for step in range(lines - 1):

        @pl.when((z - step >= 0) & (z + 1 < lines))
        def _():
            up(step, step == 0).wait_send()

        @pl.when((z + step < lines) & (z >= 1))
        def _():
            down(step, step == 0).wait_send()

    for at_z in range(lines):
        over_y(at_z).wait_send()
        for at_y in range(2):
            over_core(at_z, at_y).wait_send()
            sem = at_z * 2 + at_y
            arrived(block(at_z, at_y, 1 - core), core_recv.at[sem], core_send.at[sem])
    own_list.wait()

    @pl.loop(1, row_devices)
    def _(off):
        send_list(off).wait()

    for c in range(chunks):
        own_x(c).wait()
        for off in range(1, col_devices):

            @pl.loop(0, per_owner)
            def _(t):
                send_c(c, off, t).wait_send()

        @pl.loop(1, row_devices)
        def _(off):
            send_x(c, off).wait()


def spread(c_matrix, beta_values, beta_rows, alpha_list, flat, row_devices, col_devices, chunk):
    rows, columns = c_matrix.shape
    pairs, _, _, width, _ = beta_values.shape
    packed_shape = (flat.shape[0] * flat.shape[1] // 128, 128)
    held = columns // width
    strip, chunks = columns // row_devices, rows // chunk
    dma = pltpu.SemaphoreType.DMA
    anywhere = pl.BlockSpec(memory_space=pl.ANY)
    return pl.pallas_call(
        functools.partial(spread_kernel, chunks),
        in_specs=[
            pl.BlockSpec(memory_space=pltpu.SMEM), anywhere,
            pl.BlockSpec(memory_space=pltpu.VMEM), pl.BlockSpec(memory_space=pltpu.VMEM),
            pl.BlockSpec(memory_space=pltpu.VMEM),
        ],
        out_specs=[anywhere, anywhere, anywhere],
        out_shape=[
            jax.ShapeDtypeStruct((chunks, row_devices, pairs, strip, chunk), jnp.bfloat16),
            jax.ShapeDtypeStruct((row_devices,) + alpha_list.shape, jnp.int32),
            jax.ShapeDtypeStruct((row_devices,) + packed_shape, flat.dtype),
        ],
        scratch_shapes=[pltpu.VMEM((col_devices * columns // width, chunk, width), jnp.bfloat16)] * chunks
        + [pltpu.VMEM((pairs, columns, chunk), jnp.bfloat16)] * chunks
        + [
            dma((chunks, held)), dma((chunks, col_devices - 1, held)),
            dma((chunks, col_devices - 1, held)),
            dma((chunks, row_devices - 1)), dma((chunks, row_devices - 1)), dma((chunks,)),
            dma((row_devices - 1,)), dma((row_devices - 1,)), dma,
        ]
        + [dma((row_devices // 4 - 1,))] * 4
        + [dma((row_devices // 4,))] * 2
        + [dma((row_devices // 2,))] * 2
        + [dma, pltpu.VMEM(packed_shape, flat.dtype)],
        compiler_params=pltpu.CompilerParams(
            collective_id=0, has_side_effects=True, vmem_limit_bytes=56 << 20
        ),
        cost_estimate=pl.CostEstimate(
            flops=1 << 37, bytes_accessed=1 << 28, transcendentals=0
        ),
        name="spread",
    )(beta_rows, c_matrix, beta_values, alpha_list, flat)


def exchange_kernel(own_ref, mirror_ref, own_out, mirror_out, o_send, o_recv, m_send, m_recv, sems):
    row_devices, row = lax.axis_size("row"), lax.axis_index("row")
    col_devices, col = lax.axis_size("col"), lax.axis_index("col")

    def send_own(off):
        peer = lax.rem(row + off, row_devices)
        return remote(
            own_ref.at[peer], own_out.at[row], o_send.at[off - 1], o_recv.at[off - 1], "row", peer
        )

    def send_mirror(off):
        peer = lax.rem(col + off, col_devices)
        return remote(
            mirror_ref.at[peer], mirror_out.at[col], m_send.at[off - 1], m_recv.at[off - 1],
            "col", peer,
        )

    stay_own = pltpu.make_async_copy(own_ref.at[row], own_out.at[row], sems.at[0])
    stay_mirror = pltpu.make_async_copy(mirror_ref.at[col], mirror_out.at[col], sems.at[1])
    greet(("row", "col"))

    @pl.loop(1, col_devices)
    def _(off):
        send_mirror(off).start()

    @pl.loop(1, row_devices)
    def _(off):
        send_own(off).start()

    stay_own.start()
    stay_mirror.start()
    stay_own.wait()
    stay_mirror.wait()

    @pl.loop(1, row_devices)
    def _(off):
        send_own(off).wait()

    @pl.loop(1, col_devices)
    def _(off):
        send_mirror(off).wait()


def exchange(own, mirror):
    dma = pltpu.SemaphoreType.DMA
    anywhere = pl.BlockSpec(memory_space=pl.ANY)
    local = pl.BlockSpec(memory_space=pltpu.VMEM)
    row_devices, col_devices = own.shape[0], mirror.shape[0]
    return pl.pallas_call(
        exchange_kernel,
        in_specs=[local, local],
        out_specs=[anywhere, anywhere],
        out_shape=[
            jax.ShapeDtypeStruct(own.shape, own.dtype),
            jax.ShapeDtypeStruct(mirror.shape, mirror.dtype),
        ],
        scratch_shapes=[
            dma((row_devices - 1,)), dma((row_devices - 1,)),
            dma((col_devices - 1,)), dma((col_devices - 1,)), dma((2,)),
        ],
        compiler_params=pltpu.CompilerParams(
            collective_id=1, has_side_effects=True, vmem_limit_bytes=56 << 20
        ),
        name="exchange",
    )(own, mirror)


def per_device(c_matrix, beta_values, beta_rows, alpha_values, alpha_rows, gaps):
    row_devices, col_devices = lax.axis_size("row"), lax.axis_size("col")
    groups, stretch, columns = c_matrix.shape
    pairs, _, _, listed, tile, _ = alpha_values.shape
    rows, chunk = groups * stretch, beta_values.shape[-1]
    c_rows = c_matrix.reshape(rows, columns)
    alpha_tiles = alpha_values.reshape(pairs * groups, listed, tile, tile)
    alpha_list = alpha_rows.reshape(pairs * groups, listed)
    own_kernels = stretch % 16 == 0 and rows % chunk == 0 and tile % 128 == 64
    own_kernels = own_kernels and row_devices % 4 == 0 and pairs * groups % 2 == 0
    if own_kernels:
        entries = alpha_list.size
        padded = jnp.pad(alpha_list.reshape(-1), (0, -entries % 1024)).reshape(-1, 128)
        x_strip, rows_all, alpha_all = spread(
            c_rows, beta_values, beta_rows, padded, alpha_tiles.reshape(-1, tile), row_devices,
            col_devices, chunk,
        )
        rows_all = rows_all.reshape(row_devices, -1)[:, :entries]
        rows_all = rows_all.reshape(row_devices, pairs * groups, listed)
    else:
        rows_all = lax.all_gather(alpha_list, "row")
        alpha_all = lax.all_gather(alpha_tiles, "row")
        xt = beta_products(lax.all_gather(c_rows, "col"), beta_values, beta_rows)
        xt = jnp.moveaxis(xt.reshape(pairs, row_devices, stretch, rows), 1, 0)
        x_strip = lax.all_to_all(xt, "row", 0, 0)[None]
    own, mirror = alpha_products(alpha_all, rows_all, x_strip, groups)
    if own_kernels:
        own, mirror = exchange(own, mirror)
    else:
        own = lax.all_to_all(own, "row", 0, 0)
        mirror = lax.all_to_all(mirror, "col", 0, 0)
    out = final(
        own.reshape(columns, groups * stretch),
        mirror.reshape(groups * stretch, columns),
        gaps.reshape(groups * stretch, columns),
    )
    return out.reshape(gaps.shape)


def solution(mesh):
    placed = (
        P(None, "row", "col"),
        P(None, "col", None, None, None),
        P(None, "col", None),
        P(None, None, "row", None, None, None),
        P(None, None, "row", None),
        P(None, "row", "col"),
    )
    return jax.shard_map(
        per_device, mesh=mesh, in_specs=placed, out_specs=P(None, "row", "col"), check_vma=False
    )
```

```python
import functools

import jax
import jax.numpy as jnp
from jax import lax
from jax.experimental import pallas as pl
from jax.experimental.pallas import tpu as pltpu
from jax.sharding import PartitionSpec as P

CONTRACT_LAST = (((1,), (1,)), ((), ()))


def beta_kernel(listed, held, rows_ref, c_ref, b_ref, xt_ref):
    k, j = pl.program_id(0), pl.program_id(1)
    width = b_ref.shape[-1]
    picked = []
    for z in range(listed):
        tile = rows_ref[k, j, z]
        owner = tile // held
        start = pl.multiple_of((tile - owner * held) * width, width)
        picked.append(c_ref[owner, :, pl.ds(start, width)])
    lhs = b_ref[0, 0].reshape(listed * width, width)
    product = lax.dot_general(
        lhs, jnp.concatenate(picked, axis=1), (((0,), (1,)), ((), ())),
        preferred_element_type=jnp.float32,
    )
    xt_ref[0] = product.astype(xt_ref.dtype)


def beta_products(gathered, beta_values, beta_rows):
    pairs, tiles, listed, width, _ = beta_values.shape
    owners, rows, columns = gathered.shape
    return pl.pallas_call(
        functools.partial(beta_kernel, listed, columns // width),
        grid_spec=pltpu.PrefetchScalarGridSpec(
            num_scalar_prefetch=1,
            grid=(pairs, tiles),
            in_specs=[
                pl.BlockSpec((owners, rows, columns), lambda k, j, s: (0, 0, 0)),
                pl.BlockSpec((1, 1, listed, width, width), lambda k, j, s: (k, j, 0, 0, 0)),
            ],
            out_specs=pl.BlockSpec((1, width, rows), lambda k, j, s: (k, j, 0)),
        ),
        out_shape=jax.ShapeDtypeStruct((pairs, tiles * width, rows), jnp.bfloat16),
        compiler_params=pltpu.CompilerParams(vmem_limit_bytes=56 << 20),
        name="beta_products",
    )(beta_rows, gathered, beta_values)


def pack_alpha(flat_ref, packed_ref):
    size, tile = flat_ref.shape
    half, whole = size // 2, tile // 128
    for i in range(whole):
        packed_ref[pl.ds(i * size, size), :] = flat_ref[:, i * 128 : (i + 1) * 128]
    packed_ref[pl.ds(whole * size, half), :] = jnp.concatenate(
        [flat_ref[pl.ds(0, half), whole * 128 :], flat_ref[pl.ds(half, half), whole * 128 :]], axis=1
    )


def packed_product(a_ref, at, slot, slots, listed, tile, x):
    size, whole = listed * tile, tile // 128
    parts = [a_ref[at, pl.ds(i * slots * size + slot * size, size), :] for i in range(whole)]
    parts.append(a_ref[at, pl.ds(whole * slots * size + slot % (slots // 2) * size, size), :])
    blank = jnp.zeros((x.shape[0], 64), x.dtype)
    tail = [x[:, whole * 128 :], blank]
    if slot >= slots // 2:
        tail = tail[::-1]
    wide = jnp.concatenate([x[:, : whole * 128]] + tail, axis=1)
    return lax.dot_general(
        jnp.concatenate(parts, axis=1), wide, CONTRACT_LAST, preferred_element_type=jnp.float32
    )


def alpha_kernel(groups, rows_ref, a_ref, x_ref, own_ref, mirror_ref, acc_ref):
    r = pl.program_id(0)
    row_devices = pl.num_programs(0)
    pairs = x_ref.shape[2]
    listed, tile = rows_ref.shape[2], acc_ref.shape[1]

    @pl.when(r == 0)
    def _():
        acc_ref[...] = jnp.zeros_like(acc_ref)

    for i in range(x_ref.shape[1]):
        at = r * x_ref.shape[1] + i
        for k in range(pairs):
            parts = [x_ref[c, i, k] for c in range(x_ref.shape[0])]
            merged = jnp.concatenate(parts, axis=1) if len(parts) > 1 else parts[0]
            for g in range(groups):
                x = merged[:, g * tile : (g + 1) * tile]
                slot = k * groups + g
                if len(a_ref.shape) == 3:
                    product = packed_product(a_ref, i, slot, pairs * groups, listed, tile, x)
                    for z in range(listed):
                        acc_ref[rows_ref[at, slot, z]] += product[z * tile : (z + 1) * tile]
                else:

                    @pl.loop(0, listed)
                    def _(z):
                        acc_ref[rows_ref[at, slot, z]] += lax.dot_general(
                            a_ref[i, slot, z], x, CONTRACT_LAST,
                            preferred_element_type=jnp.float32,
                        )

    @pl.when(r == row_devices - 1)
    def _():
        count = acc_ref.shape[0] // groups
        for g in range(groups):
            for to in range(count):
                turned = acc_ref[g * count + to].astype(own_ref.dtype).T
                own_ref[to, :, g * tile : (g + 1) * tile] = turned
                mirror_ref[g, :, to * tile : (to + 1) * tile] = turned


def alpha_products(alpha_all, rows_all, x_strip, groups):
    row_devices, rest = alpha_all.shape[0], alpha_all.shape[1:]
    tile = x_strip.shape[0] * x_strip.shape[-1] // groups
    per = 4 if len(rest) == 2 and row_devices % 4 == 0 else 1
    chunks, _, pairs, strip, chunk = x_strip.shape
    return pl.pallas_call(
        functools.partial(alpha_kernel, groups),
        grid_spec=pltpu.PrefetchScalarGridSpec(
            num_scalar_prefetch=1,
            grid=(row_devices // per,),
            in_specs=[
                pl.BlockSpec((per,) + rest, lambda r, s: (r,) + (0,) * len(rest)),
                pl.BlockSpec((chunks, per, pairs, strip, chunk), lambda r, s: (0, r, 0, 0, 0)),
            ],
            out_specs=[
                pl.BlockSpec((row_devices, strip, groups * tile), lambda r, s: (0, 0, 0)),
                pl.BlockSpec((groups, strip, row_devices * tile), lambda r, s: (0, 0, 0)),
            ],
            scratch_shapes=[pltpu.VMEM((groups * row_devices, tile, strip), jnp.float32)],
        ),
        out_shape=[
            jax.ShapeDtypeStruct((row_devices, strip, groups * tile), jnp.bfloat16),
            jax.ShapeDtypeStruct((groups, strip, row_devices * tile), jnp.bfloat16),
        ],
        compiler_params=pltpu.CompilerParams(vmem_limit_bytes=56 << 20),
        name="alpha_products",
    )(rows_all, alpha_all, x_strip)


def final_kernel(own_ref, mirror_ref, gaps_ref, out_ref):
    own = own_ref[...].T.astype(jnp.float32)
    out_ref[...] = (own + mirror_ref[...].astype(jnp.float32)) / gaps_ref[...]


def final(own, mirror, gaps):
    rows, columns = gaps.shape
    block = next(n for n in (384, 256, 128) if columns % n == 0)
    wide = pl.BlockSpec((rows, block), lambda i: (0, i))
    return pl.pallas_call(
        final_kernel,
        grid=(columns // block,),
        in_specs=[pl.BlockSpec((block, rows), lambda i: (i, 0)), wide, wide],
        out_specs=wide,
        out_shape=jax.ShapeDtypeStruct((rows, columns), jnp.float32),
        name="final",
    )(own, mirror, gaps)


def greet(axes):
    barrier = pltpu.get_barrier_semaphore()
    total = 0
    for axis in axes:
        size, me = lax.axis_size(axis), lax.axis_index(axis)
        total += size - 1

        @pl.loop(1, size)
        def _(off):
            pl.semaphore_signal(
                barrier, inc=1, device_id={axis: lax.rem(me + off, size)},
                device_id_type=pl.DeviceIdType.MESH,
            )

    pl.semaphore_wait(barrier, total)


def alternate(step, size):
    odd = lax.rem(step, 2)
    return odd * ((step + 1) // 2) + (1 - odd) * (size - step // 2)


def remote(src, dst, send_sem, recv_sem, axis, peer):
    return pltpu.make_async_remote_copy(
        src_ref=src, dst_ref=dst, send_sem=send_sem, recv_sem=recv_sem,
        device_id={axis: peer}, device_id_type=pl.DeviceIdType.MESH,
    )


def spread_kernel(chunks, rows_ref, c_ref, b_ref, list_ref, flat_ref, x_ref, lists_ref, all_ref, *scratch):
    held, sent = scratch[:chunks], scratch[chunks : 2 * chunks]
    (local_sem, c_send, c_recv, x_send, x_recv, own_sem, l_send, l_recv, l_own, up_send, up_recv,
     down_send, down_recv, y_send, y_recv, core_send, core_recv, a_own, a_ref) = scratch[2 * chunks :]
    row_devices, row = lax.axis_size("row"), lax.axis_index("row")
    col_devices, col = lax.axis_size("col"), lax.axis_index("col")
    pairs, tiles, listed, width, _ = b_ref.shape
    rows, columns = c_ref.shape
    per_owner = columns // width
    chunk = rows // chunks
    strip = per_owner * width // row_devices

    def own_c(c, t):
        return pltpu.make_async_copy(
            c_ref.at[pl.ds(c * chunk, chunk), pl.ds(pl.multiple_of(t * width, width), width)],
            held[c].at[col * per_owner + t], local_sem.at[c, t],
        )

    def send_c(c, off, t):
        return remote(
            c_ref.at[pl.ds(c * chunk, chunk), pl.ds(pl.multiple_of(t * width, width), width)],
            held[c].at[col * per_owner + t], c_send.at[c, off - 1, t], c_recv.at[c, off - 1, t],
            "col", lax.rem(col + off, col_devices),
        )

    def send_x(c, off):
        peer = lax.rem(row + off, row_devices)
        start = pl.multiple_of(peer * strip, 16)
        return remote(
            sent[c].at[:, pl.ds(start, strip), :], x_ref.at[c, row], x_send.at[c, off - 1],
            x_recv.at[c, off - 1], "row", peer,
        )

    def own_x(c):
        start = pl.multiple_of(row * strip, 16)
        return pltpu.make_async_copy(
            sent[c].at[:, pl.ds(start, strip), :], x_ref.at[c, row], own_sem.at[c]
        )

    def send_list(off):
        return remote(
            list_ref, lists_ref.at[row], l_send.at[off - 1], l_recv.at[off - 1], "row",
            lax.rem(row + off, row_devices),
        )

    lines = row_devices // 4
    z, y, core = row // 4, lax.rem(row // 2, 2), lax.rem(row, 2)

    def block(at_z, at_y, at_core):
        return (at_z * 2 + at_y) * 2 + at_core

    def hand(source, at, send_sem, recv_sem, peer):
        return remote(source, all_ref.at[at], send_sem, recv_sem, "row", peer)

    def up(step, first=False):
        at = block(z - step, y, core)
        source = a_ref if first else all_ref.at[at]
        return hand(source, at, up_send.at[step], up_recv.at[step], block(z + 1, y, core))

    def down(step, first=False):
        at = block(z + step, y, core)
        source = a_ref if first else all_ref.at[at]
        return hand(source, at, down_send.at[step], down_recv.at[step], block(z - 1, y, core))

    def over_y(at_z, first=False):
        at = block(at_z, y, core)
        source = a_ref if first else all_ref.at[at]
        return hand(source, at, y_send.at[at_z], y_recv.at[at_z], block(z, 1 - y, core))

    def over_core(at_z, at_y, first=False):
        at = block(at_z, at_y, core)
        source = a_ref if first else all_ref.at[at]
        sem = at_z * 2 + at_y
        return hand(source, at, core_send.at[sem], core_recv.at[sem], block(z, y, 1 - core))

    def arrived(at, recv_sem, send_sem):
        hand(all_ref.at[at], at, send_sem, recv_sem, block(z, y, 1 - core)).wait_recv()

    def relay(step):
        @pl.when(z - 1 - step >= 0)
        def _():
            arrived(block(z - 1 - step, y, core), up_recv.at[step], up_send.at[step])
            if step + 1 < lines - 1:

                @pl.when(z + 1 < lines)
                def _():
                    up(step + 1).start()

            over_y(z - 1 - step).start()
            over_core(z - 1 - step, y).start()

        @pl.when(z + 1 + step < lines)
        def _():
            arrived(block(z + 1 + step, y, core), down_recv.at[step], down_send.at[step])
            if step + 1 < lines - 1:

                @pl.when(z >= 1)
                def _():
                    down(step + 1).start()

            over_y(z + 1 + step).start()
            over_core(z + 1 + step, y).start()

    def cross(step):
        at_z = lax.rem(z + step, lines)
        arrived(block(at_z, 1 - y, core), y_recv.at[at_z], y_send.at[at_z])
        over_core(at_z, 1 - y).start()

    own_a = pltpu.make_async_copy(a_ref, all_ref.at[row], a_own)
    own_list = pltpu.make_async_copy(list_ref, lists_ref.at[row], l_own)
    for c in range(chunks):

        @pl.loop(0, per_owner)
        def _(t):
            own_c(c, t).start()

    own_list.start()
    pack_alpha(flat_ref, a_ref)
    greet(("row", "col"))
    for c in range(chunks):
        for off in range(1, col_devices):

            @pl.loop(0, per_owner)
            def _(t):
                send_c(c, off, t).start()

    @pl.when(z + 1 < lines)
    def _():
        up(0, True).start()

    @pl.when(z >= 1)
    def _():
        down(0, True).start()

    over_y(z, True).start()
    over_core(z, y, True).start()
    own_a.start()

    @pl.loop(1, row_devices)
    def _(off):
        send_list(off).start()

    relayed = 0
    for c in range(chunks):
        if relayed < lines - 1:
            relay(relayed)
            relayed += 1

        @pl.loop(0, per_owner)
        def _(t):
            own_c(c, t).wait()
            for off in range(1, col_devices):
                send_c(c, off, t).wait_recv()

        @pl.loop(0, tiles)
        def _(j):
            for k in range(pairs):
                picked = [held[c][rows_ref[k, j, z]] for z in range(listed)]
                product = lax.dot_general(
                    b_ref[k, j].reshape(listed * width, width), jnp.concatenate(picked, axis=1),
                    (((0,), (1,)), ((), ())), preferred_element_type=jnp.float32,
                )
                sent[c][k, pl.ds(pl.multiple_of(j * width, width), width), :] = product.astype(
                    jnp.bfloat16
                )

        @pl.loop(1, row_devices)
        def _(off):
            send_x(c, alternate(off, row_devices)).start()

        own_x(c).start()
        if c == 0:
            cross(0)

    for step in range(relayed, lines - 1):
        relay(step)
    for step in range(1, lines):
        cross(step)
    own_a.wait()
    for step in range(lines - 1):

        @pl.when((z - step >= 0) & (z + 1 < lines))
        def _():
            up(step, step == 0).wait_send()

        @pl.when((z + step < lines) & (z >= 1))
        def _():
            down(step, step == 0).wait_send()

    for at_z in range(lines):
        over_y(at_z).wait_send()
        for at_y in range(2):
            over_core(at_z, at_y).wait_send()
            sem = at_z * 2 + at_y
            arrived(block(at_z, at_y, 1 - core), core_recv.at[sem], core_send.at[sem])
    own_list.wait()

    @pl.loop(1, row_devices)
    def _(off):
        send_list(off).wait()

    for c in range(chunks):
        own_x(c).wait()
        for off in range(1, col_devices):

            @pl.loop(0, per_owner)
            def _(t):
                send_c(c, off, t).wait_send()

        @pl.loop(1, row_devices)
        def _(off):
            send_x(c, off).wait()


def spread(c_matrix, beta_values, beta_rows, alpha_list, flat, row_devices, col_devices, chunk):
    rows, columns = c_matrix.shape
    pairs, _, _, width, _ = beta_values.shape
    packed_shape = (flat.shape[0] * flat.shape[1] // 128, 128)
    held = columns // width
    strip, chunks = columns // row_devices, rows // chunk
    dma = pltpu.SemaphoreType.DMA
    anywhere = pl.BlockSpec(memory_space=pl.ANY)
    return pl.pallas_call(
        functools.partial(spread_kernel, chunks),
        in_specs=[
            pl.BlockSpec(memory_space=pltpu.SMEM), anywhere,
            pl.BlockSpec(memory_space=pltpu.VMEM), pl.BlockSpec(memory_space=pltpu.VMEM),
            pl.BlockSpec(memory_space=pltpu.VMEM),
        ],
        out_specs=[anywhere, anywhere, anywhere],
        out_shape=[
            jax.ShapeDtypeStruct((chunks, row_devices, pairs, strip, chunk), jnp.bfloat16),
            jax.ShapeDtypeStruct((row_devices,) + alpha_list.shape, jnp.int32),
            jax.ShapeDtypeStruct((row_devices,) + packed_shape, flat.dtype),
        ],
        scratch_shapes=[pltpu.VMEM((col_devices * columns // width, chunk, width), jnp.bfloat16)] * chunks
        + [pltpu.VMEM((pairs, columns, chunk), jnp.bfloat16)] * chunks
        + [
            dma((chunks, held)), dma((chunks, col_devices - 1, held)),
            dma((chunks, col_devices - 1, held)),
            dma((chunks, row_devices - 1)), dma((chunks, row_devices - 1)), dma((chunks,)),
            dma((row_devices - 1,)), dma((row_devices - 1,)), dma,
        ]
        + [dma((row_devices // 4 - 1,))] * 4
        + [dma((row_devices // 4,))] * 2
        + [dma((row_devices // 2,))] * 2
        + [dma, pltpu.VMEM(packed_shape, flat.dtype)],
        compiler_params=pltpu.CompilerParams(
            collective_id=0, has_side_effects=True, vmem_limit_bytes=56 << 20
        ),
        cost_estimate=pl.CostEstimate(
            flops=1 << 37, bytes_accessed=1 << 28, transcendentals=0
        ),
        name="spread",
    )(beta_rows, c_matrix, beta_values, alpha_list, flat)


def exchange_kernel(own_ref, mirror_ref, own_out, mirror_out, o_send, o_recv, m_send, m_recv, sems):
    row_devices, row = lax.axis_size("row"), lax.axis_index("row")
    col_devices, col = lax.axis_size("col"), lax.axis_index("col")

    def send_own(off):
        peer = lax.rem(row + off, row_devices)
        return remote(
            own_ref.at[peer], own_out.at[row], o_send.at[off - 1], o_recv.at[off - 1], "row", peer
        )

    def send_mirror(off):
        peer = lax.rem(col + off, col_devices)
        return remote(
            mirror_ref.at[peer], mirror_out.at[col], m_send.at[off - 1], m_recv.at[off - 1],
            "col", peer,
        )

    stay_own = pltpu.make_async_copy(own_ref.at[row], own_out.at[row], sems.at[0])
    stay_mirror = pltpu.make_async_copy(mirror_ref.at[col], mirror_out.at[col], sems.at[1])
    greet(("row", "col"))

    @pl.loop(1, col_devices)
    def _(off):
        send_mirror(off).start()

    @pl.loop(1, row_devices)
    def _(off):
        send_own(alternate(off, row_devices)).start()

    stay_own.start()
    stay_mirror.start()
    stay_own.wait()
    stay_mirror.wait()

    @pl.loop(1, row_devices)
    def _(off):
        send_own(off).wait()

    @pl.loop(1, col_devices)
    def _(off):
        send_mirror(off).wait()


def exchange(own, mirror):
    dma = pltpu.SemaphoreType.DMA
    anywhere = pl.BlockSpec(memory_space=pl.ANY)
    local = pl.BlockSpec(memory_space=pltpu.VMEM)
    row_devices, col_devices = own.shape[0], mirror.shape[0]
    return pl.pallas_call(
        exchange_kernel,
        in_specs=[local, local],
        out_specs=[anywhere, anywhere],
        out_shape=[
            jax.ShapeDtypeStruct(own.shape, own.dtype),
            jax.ShapeDtypeStruct(mirror.shape, mirror.dtype),
        ],
        scratch_shapes=[
            dma((row_devices - 1,)), dma((row_devices - 1,)),
            dma((col_devices - 1,)), dma((col_devices - 1,)), dma((2,)),
        ],
        compiler_params=pltpu.CompilerParams(
            collective_id=1, has_side_effects=True, vmem_limit_bytes=56 << 20
        ),
        name="exchange",
    )(own, mirror)


def per_device(c_matrix, beta_values, beta_rows, alpha_values, alpha_rows, gaps):
    row_devices, col_devices = lax.axis_size("row"), lax.axis_size("col")
    groups, stretch, columns = c_matrix.shape
    pairs, _, _, listed, tile, _ = alpha_values.shape
    rows, chunk = groups * stretch, beta_values.shape[-1]
    c_rows = c_matrix.reshape(rows, columns)
    alpha_tiles = alpha_values.reshape(pairs * groups, listed, tile, tile)
    alpha_list = alpha_rows.reshape(pairs * groups, listed)
    own_kernels = stretch % 16 == 0 and rows % chunk == 0 and tile % 128 == 64
    own_kernels = own_kernels and row_devices % 4 == 0 and pairs * groups % 2 == 0
    if own_kernels:
        entries = alpha_list.size
        padded = jnp.pad(alpha_list.reshape(-1), (0, -entries % 1024)).reshape(-1, 128)
        x_strip, rows_all, alpha_all = spread(
            c_rows, beta_values, beta_rows, padded, alpha_tiles.reshape(-1, tile), row_devices,
            col_devices, chunk,
        )
        rows_all = rows_all.reshape(row_devices, -1)[:, :entries]
        rows_all = rows_all.reshape(row_devices, pairs * groups, listed)
    else:
        rows_all = lax.all_gather(alpha_list, "row")
        alpha_all = lax.all_gather(alpha_tiles, "row")
        xt = beta_products(lax.all_gather(c_rows, "col"), beta_values, beta_rows)
        xt = jnp.moveaxis(xt.reshape(pairs, row_devices, stretch, rows), 1, 0)
        x_strip = lax.all_to_all(xt, "row", 0, 0)[None]
    own, mirror = alpha_products(alpha_all, rows_all, x_strip, groups)
    if own_kernels:
        own, mirror = exchange(own, mirror)
    else:
        own = lax.all_to_all(own, "row", 0, 0)
        mirror = lax.all_to_all(mirror, "col", 0, 0)
    out = final(
        own.reshape(columns, groups * stretch),
        mirror.reshape(groups * stretch, columns),
        gaps.reshape(groups * stretch, columns),
    )
    return out.reshape(gaps.shape)


def solution(mesh):
    placed = (
        P(None, "row", "col"),
        P(None, "col", None, None, None),
        P(None, "col", None),
        P(None, None, "row", None, None, None),
        P(None, None, "row", None),
        P(None, "row", "col"),
    )
    return jax.shard_map(
        per_device, mesh=mesh, in_specs=placed, out_specs=P(None, "row", "col"), check_vma=False
    )
```
